32 devices in a mesh: ctx: 4 (over z), fsdp: 2 (over core), kvh: 4 (over y, x).
Axes of the slice: x: 2, y: 2, z: 4, core: 2. Of those that a mesh axis runs over, the one named last changes fastest.
Arguments:
- hidden: bfloat16 [2048, 4096], P(('ctx', 'fsdp'), 'kvh'), may hold values from -6 to 6
- key_value_matrix: bfloat16 [4096, 2048], P('fsdp', 'kvh'), may hold values from -0.09375 to 0.09375
- queries: bfloat16 [2048, 4096], P(('ctx', 'fsdp'), 'kvh')
- vertical_blocks: int32 [8, 8], P('kvh'), may hold values from 0 to 15, as said below
- slash_offsets: int32 [8, 2], P('kvh'), may hold values from 1 to 15, as said below
Outputs:
- attended: bfloat16 [2048, 4096], P(('ctx', 'fsdp'), 'kvh')
The draws below stay inside these ranges and needn't reach their ends.
Inputs may be any that keep to these rules, and one draw needn't show every extreme that they name: `vertical_blocks`: the 8 entries of one head are distinct key blocks. `slash_offsets`: the 2 entries of one head are distinct block distances.
All inputs are finite; a program needn't handle non-finite values.
Results may differ from the reference program's by a relative error of at most 0.012.
The reference program's roundings to bfloat16 on the way (of `keys`, `values` and `probs`) count: a program that leaves them out, or rounds other values in their place, can miss the bound.
Values may be sent and summed in bfloat16 or wider, within the bound.
No kernel may reach another device: no remote copies, remote signals or barrier semaphores. Data moves between devices by JAX's collectives and lax.ppermute only.
A program may use at most 64 MiB of HBM per device.

```python
import jax
import jax.numpy as jnp
from jax import lax

MODEL_WIDTH = 4096
HQ = 32
KEY_VALUE_HEADS = 8
HEAD_DIMENSION = 128
BLOCK_TOKENS = 128
NS = 2
QUERY_GROUP = 4
PROMPT_BLOCKS = 16
L = 2048
NV = 8


def draw_queries(key, part):
    first_key = jax.random.fold_in(key, 0)
    base = jnp.clip(jax.random.normal(first_key, (L, HQ * HEAD_DIMENSION), jnp.float32), -6.0, 6.0)
    return (base * 1.5).astype(jnp.bfloat16)


def draw_vertical_blocks(key, part):
    per_head_keys = jax.random.split(key, KEY_VALUE_HEADS)
    picked = jax.vmap(lambda head_key: jax.random.permutation(head_key, PROMPT_BLOCKS)[:NV])(per_head_keys)
    first_key = jax.random.fold_in(key, 11)
    middle = jax.random.permutation(first_key, PROMPT_BLOCKS - 2)[:NV - 2] + 1
    ends = jnp.array([0, PROMPT_BLOCKS - 1], dtype=jnp.int32)
    first_row = jnp.concatenate([ends, middle.astype(jnp.int32)])
    picked = picked.astype(jnp.int32).at[0].set(first_row)
    return picked.astype(jnp.int32)


def draw_slash_offsets(key, part):
    per_head_keys = jax.random.split(jax.random.fold_in(key, 7), KEY_VALUE_HEADS)
    picked = jax.vmap(lambda head_key: jax.random.permutation(head_key, PROMPT_BLOCKS - 1)[:NS])(per_head_keys)
    picked = (picked + 1).astype(jnp.int32)
    first_key = jax.random.fold_in(key, 13)
    middle = jax.random.permutation(first_key, PROMPT_BLOCKS - 3)[:NS - 2] + 2
    ends = jnp.array([1, PROMPT_BLOCKS - 1], dtype=jnp.int32)
    first_row = jnp.concatenate([ends, middle.astype(jnp.int32)])
    picked = picked.at[0].set(first_row)
    return picked.astype(jnp.int32)


def levels(own_key, extent, cuts, low, high):
    def one(dim, shards_of):
        steps = jax.random.uniform(jax.random.fold_in(jax.random.fold_in(own_key, 6), dim), (shards_of,), jnp.float32, low / len(cuts), high / len(cuts))
        return jnp.repeat(jnp.exp(steps), extent[dim] // shards_of).reshape((-1,) + (1,) * (len(extent) - dim - 1))

    loudness = one(*cuts[0])
    for cut in cuts[1:]:
        loudness = loudness * one(*cut)
    return loudness


def centred(own_key, dims, width, bound, shards=(), kind=jnp.bfloat16):
    factor_of = levels(own_key, dims, shards, -0.22, 0.18) if shards else 1.0
    values = jax.random.normal(own_key, dims, jnp.float32) * width * factor_of
    return jnp.minimum(jnp.maximum(values, -bound), bound).astype(kind)


def setup_inputs(seed: int = 0) -> dict:
    keys = jax.random.split(jax.random.key(seed), 6)
    hidden = centred(keys[0], (L, MODEL_WIDTH), 1.0, 6.0, ((0, 8), (1, 4)))
    key_value_matrix = centred(keys[1], (MODEL_WIDTH, 2 * KEY_VALUE_HEADS * HEAD_DIMENSION), MODEL_WIDTH ** -0.5, 0.09375, ((0, 2), (1, 4)))
    queries = draw_queries(jax.random.fold_in(keys[5], 71), 0)
    vertical_blocks = draw_vertical_blocks(jax.random.fold_in(keys[5], 71), 0)
    slash_offsets = draw_slash_offsets(jax.random.fold_in(keys[5], 71), 0)
    return dict(hidden=hidden, key_value_matrix=key_value_matrix, queries=queries, vertical_blocks=vertical_blocks, slash_offsets=slash_offsets)


def rotate_keys(raw_keys, positions):
    half = HEAD_DIMENSION // 2
    frequency = jnp.power(500000.0, -(jnp.arange(half, dtype=jnp.float32) * 2.0 / HEAD_DIMENSION))
    angle = positions[:, None] * frequency[None, :]
    cosine = jnp.cos(angle)[:, None, :]
    sine = jnp.sin(angle)[:, None, :]
    first_half = raw_keys[..., :half]
    second_half = raw_keys[..., half:]
    return jnp.concatenate([first_half * cosine - second_half * sine, second_half * cosine + first_half * sine], axis=-1)


def reference(hidden, key_value_matrix, queries, vertical_blocks, slash_offsets):
    total_sum = hidden.shape[0]
    projected_tokens = jnp.dot(hidden, key_value_matrix, preferred_element_type=jnp.float32).reshape(total_sum, KEY_VALUE_HEADS, 2, HEAD_DIMENSION)
    positions = jnp.arange(total_sum, dtype=jnp.float32)
    key_tensor = rotate_keys(projected_tokens[:, :, 0], positions).astype(jnp.bfloat16)
    value_tensor = projected_tokens[:, :, 1].astype(jnp.bfloat16)
    blocked_keys = key_tensor.reshape(PROMPT_BLOCKS, BLOCK_TOKENS, KEY_VALUE_HEADS, HEAD_DIMENSION).transpose(2, 0, 1, 3)
    blocked_values = value_tensor.reshape(PROMPT_BLOCKS, BLOCK_TOKENS, KEY_VALUE_HEADS, HEAD_DIMENSION).transpose(2, 0, 1, 3)
    per_head_rows = jnp.arange(KEY_VALUE_HEADS, dtype=jnp.int32)[:, None]
    slots = 1 + NV + NS
    slot_ids = jnp.arange(slots, dtype=jnp.int32)
    token_ids = jnp.arange(BLOCK_TOKENS, dtype=jnp.int32)
    token_ok = (slot_ids[None, :, None] > 0) | (token_ids[None, None, :] <= token_ids[:, None, None])
    scale = HEAD_DIMENSION ** -0.5

    def one_block(mask_block):
        own_diagonal = jnp.full((KEY_VALUE_HEADS, 1), mask_block, dtype=jnp.int32)
        slash_ids = mask_block - slash_offsets
        chosen = jnp.concatenate([own_diagonal, vertical_blocks.astype(jnp.int32), slash_ids.astype(jnp.int32)], axis=1)
        vertical_allowed = (vertical_blocks < mask_block) & jnp.logical_not(jnp.any((mask_block - vertical_blocks)[:, :, None] == slash_offsets[:, None, :], axis=-1))
        slash_allowed = slash_offsets <= mask_block
        valid_mask = jnp.concatenate([jnp.ones((KEY_VALUE_HEADS, 1), dtype=bool), vertical_allowed, slash_allowed], axis=1)
        clipped = jnp.clip(chosen, 0, PROMPT_BLOCKS - 1)
        key_sel = blocked_keys[per_head_rows, clipped]
        value_sel = blocked_values[per_head_rows, clipped]
        current_query_block = lax.dynamic_slice_in_dim(queries, (mask_block * BLOCK_TOKENS).astype(jnp.int32), BLOCK_TOKENS, 0).reshape(BLOCK_TOKENS, KEY_VALUE_HEADS, QUERY_GROUP, HEAD_DIMENSION)
        scores = jnp.einsum("thgd,hsud->hgtsu", current_query_block.astype(jnp.float32), key_sel.astype(jnp.float32)) * scale
        allowed = valid_mask[:, None, None, :, None] & token_ok[None, None]
        scores = jnp.where(allowed, scores, -jnp.inf)
        largest = jnp.max(scores, axis=(3, 4), keepdims=True)
        expo = jnp.exp(scores - largest)
        probs = (expo / jnp.sum(expo, axis=(3, 4), keepdims=True)).astype(jnp.bfloat16)
        result = jnp.einsum("hgtsu,hsud->thgd", probs.astype(jnp.float32), value_sel.astype(jnp.float32))
        return result.astype(jnp.bfloat16).reshape(BLOCK_TOKENS, HQ * HEAD_DIMENSION)

    outputs = lax.map(one_block, jnp.arange(PROMPT_BLOCKS, dtype=jnp.int32))
    return outputs.reshape(total_sum, HQ * HEAD_DIMENSION)
```

```python
import functools

import jax
import jax.numpy as jnp
from jax import lax
from jax.experimental import pallas as pl
from jax.experimental.pallas import tpu as pltpu
from jax.sharding import PartitionSpec as P

HEAD_DIMENSION = 128
BLOCK_TOKENS = 128
LOG2_E = 1.4426950408889634


ANY = pl.BlockSpec(memory_space=pl.ANY)
VMEM = pl.BlockSpec(memory_space=pltpu.VMEM)
SMEM = pl.BlockSpec(memory_space=pltpu.SMEM)


def swap(value, axis, bit):
    size = lax.axis_size(axis)
    return lax.ppermute(value, axis, [(i, i ^ bit) for i in range(size)])


def forward(value, axis):
    size = lax.axis_size(axis)
    return lax.ppermute(value, axis, [(i, i + 1) for i in range(size - 1)])


def rotary_tables(positions):
    half = HEAD_DIMENSION // 2
    frequency = jnp.power(
        500000.0, -(jnp.arange(half, dtype=jnp.float32) * 2.0 / HEAD_DIMENSION)
    )
    angle = positions[:, None] * frequency[None, :]
    cosine = jnp.cos(angle)
    sine = jnp.sin(angle)
    return (
        jnp.concatenate([cosine, cosine], axis=1),
        jnp.concatenate([-sine, sine], axis=1),
    )


def project_kernel(
    where_ref, own_ref, by_one_ref, by_two_ref, top_ref, bottom_ref,
    weight_ref, other_weight_ref, cosine_ref, sine_ref, out_ref, total_ref,
):
    kvh = where_ref[0]
    fsdp = where_ref[1]
    width = own_ref.shape[1]
    per_half = weight_ref.shape[0] // width
    rows = own_ref.shape[0]

    def add(piece, bits, weights, row0, first=False):
        chunk = kvh ^ bits
        start = pl.multiple_of((chunk % per_half) * width, width)
        product = jnp.dot(
            piece, weights[pl.ds(start, width), :], preferred_element_type=jnp.float32
        )
        span = pl.ds(row0, piece.shape[0])
        if first:
            total_ref[span, :] = product
        else:
            total_ref[span, :] += product

    def accumulate(near, far):
        add(own_ref[...], 0, near, 0, first=True)
        add(by_one_ref[...], 1, near, 0)
        add(by_two_ref[...], 2, far, 0)
        add(top_ref[...], 3, far, 0)
        add(bottom_ref[...], 3, far, rows // 2)

    near_is_own = (kvh // per_half) == fsdp

    @pl.when(near_is_own)
    def _():
        accumulate(weight_ref, other_weight_ref)

    @pl.when(jnp.logical_not(near_is_own))
    def _():
        accumulate(other_weight_ref, weight_ref)

    size = HEAD_DIMENSION
    for head in range(out_ref.shape[1] // (2 * size)):
        at = 2 * head * size
        key = total_ref[:, at : at + size]
        turned = key * cosine_ref[...] + pltpu.roll(key, size // 2, 1) * sine_ref[...]
        out_ref[:, at : at + size] = turned.astype(out_ref.dtype)
        value = total_ref[:, at + size : at + 2 * size]
        out_ref[:, at + size : at + 2 * size] = value.astype(out_ref.dtype)


def project(where, pieces, weight, other_weight, cosine, sine):
    rows = pieces[0].shape[0]
    columns = weight.shape[1]
    return pl.pallas_call(
        project_kernel,
        out_shape=jax.ShapeDtypeStruct((rows, columns), jnp.bfloat16),
        in_specs=[SMEM] + [VMEM] * 9,
        out_specs=VMEM,
        scratch_shapes=[pltpu.VMEM((rows, columns), jnp.float32)],
        cost_estimate=pl.CostEstimate(
            flops=2 * rows * columns * 2 * weight.shape[0],
            bytes_accessed=4 * weight.size + 8 * rows * columns,
            transcendentals=0,
        ),
    )(where, *pieces, weight, other_weight, cosine, sine)


def attend_kernel(
    piece_count, where_ref, vertical_ref, slash_ref, query_ref, *refs
):
    piece_refs = refs[:piece_count]
    out_ref, kv_ref, key_ref, value_ref, sem = refs[piece_count:]
    size = HEAD_DIMENSION
    block = BLOCK_TOKENS
    position = where_ref[0]
    copies = [
        pltpu.make_async_copy(
            piece, kv_ref.at[pl.ds(pl.multiple_of(where_ref[1 + n], block), piece.shape[0])], sem.at[n]
        )
        for n, piece in enumerate(piece_refs)
    ]
    for copy in copies:
        copy.start()
    for copy in copies:
        copy.wait()
    heads = kv_ref.shape[1] // (2 * size)
    group = query_ref.shape[1] // (heads * size)
    vertical_count = vertical_ref.shape[1]
    slash_count = slash_ref.shape[1]
    local_count = query_ref.shape[0] // block
    factor = size ** (-0.5) * LOG2_E
    lower = lax.broadcasted_iota(jnp.int32, (block, block), 1) <= lax.broadcasted_iota(
        jnp.int32, (block, block), 0
    )
    for local in range(local_count):
        mask_block = position * local_count + local
        for head in range(heads):
            offsets = [slash_ref[head, n] for n in range(slash_count)]
            slots = [(mask_block, None)]
            for n in range(vertical_count):
                wanted = vertical_ref[head, n]
                valid = wanted < mask_block
                for offset in offsets:
                    valid = jnp.logical_and(valid, mask_block - wanted != offset)
                slots.append((wanted, valid))
            for offset in offsets:
                valid = offset <= mask_block
                slots.append((jnp.where(valid, mask_block - offset, 0), valid))
            for n, (wanted, _) in enumerate(slots):
                start = pl.multiple_of(wanted * block, block)
                both = kv_ref[pl.ds(start, block), 2 * head * size : 2 * (head + 1) * size]
                key_ref[n * block : (n + 1) * block, :] = both[:, :size]
                value_ref[n * block : (n + 1) * block, :] = both[:, size:]
            bias = [
                None if valid is None else jnp.where(valid, 0.0, -jnp.inf).astype(jnp.float32)
                for _, valid in slots
            ]
            for member in range(group):
                at = (head * group + member) * size
                query = query_ref[local * block : (local + 1) * block, at : at + size]
                scores = lax.dot_general(
                    query, key_ref[...], (((1,), (1,)), ((), ())),
                    preferred_element_type=jnp.float32,
                )
                parts = [
                    jnp.where(lower, scores[:, :block], -jnp.inf)
                    if bias[n] is None
                    else scores[:, n * block : (n + 1) * block] + bias[n]
                    for n in range(len(slots))
                ]
                largest = functools.reduce(jnp.maximum, parts)
                largest = jnp.max(largest, axis=1, keepdims=True) * factor
                expo = [jnp.exp2(part * factor - largest) for part in parts]
                total = jnp.sum(functools.reduce(jnp.add, expo), axis=1, keepdims=True)
                probs = jnp.concatenate([part.astype(jnp.bfloat16) for part in expo], axis=1)
                result = jnp.dot(probs, value_ref[...], preferred_element_type=jnp.float32)
                out_ref[local * block : (local + 1) * block, at : at + size] = (
                    result / total
                ).astype(out_ref.dtype)


def attend(where, vertical_blocks, slash_offsets, queries, pieces):
    rows = queries.shape[0]
    columns = pieces[0].shape[1]
    total_rows = sum(piece.shape[0] for piece in pieces)
    slots = 1 + vertical_blocks.shape[1] + slash_offsets.shape[1]
    keys = slots * BLOCK_TOKENS
    return pl.pallas_call(
        functools.partial(attend_kernel, len(pieces)),
        out_shape=jax.ShapeDtypeStruct(queries.shape, jnp.bfloat16),
        in_specs=[SMEM, SMEM, SMEM, VMEM] + [ANY] * len(pieces),
        out_specs=VMEM,
        scratch_shapes=[
            pltpu.VMEM((total_rows, columns), jnp.bfloat16),
            pltpu.VMEM((keys, HEAD_DIMENSION), jnp.bfloat16),
            pltpu.VMEM((keys, HEAD_DIMENSION), jnp.bfloat16),
            pltpu.SemaphoreType.DMA((len(pieces),)),
        ],
        compiler_params=pltpu.CompilerParams(vmem_limit_bytes=60 << 20),
        cost_estimate=pl.CostEstimate(
            flops=4 * rows * queries.shape[1] * keys,
            bytes_accessed=2 * total_rows * columns + 4 * queries.size,
            transcendentals=rows * keys * queries.shape[1] // HEAD_DIMENSION,
        ),
    )(where, vertical_blocks, slash_offsets, queries, *pieces)


def per_device(hidden, key_value_matrix, queries, vertical_blocks, slash_offsets):
    rows = hidden.shape[0]
    half_rows = rows // 2
    kvh = lax.axis_index("kvh")
    fsdp = lax.axis_index("fsdp")
    ctx = lax.axis_index("ctx")
    ctx_size = lax.axis_size("ctx")
    fsdp_size = lax.axis_size("fsdp")
    position = ctx * fsdp_size + fsdp

    other_weight = swap(key_value_matrix, "fsdp", 1)
    by_one = swap(hidden, "kvh", 1)
    by_two = swap(hidden, "kvh", 2)
    top = swap(by_one[:half_rows], "kvh", 2)
    bottom = swap(by_two[half_rows:], "kvh", 1)

    positions = (position * rows + jnp.arange(rows, dtype=jnp.int32)).astype(jnp.float32)
    cosine, sine = rotary_tables(positions)
    kv = project(
        jnp.stack([kvh, fsdp]), (hidden, by_one, by_two, top, bottom),
        key_value_matrix, other_weight, cosine, sine,
    )
    if ctx_size <= 4:
        pieces = []
        places = []
        moving = kv
        for step in range(ctx_size):
            if step:
                moving = forward(moving, "ctx")
            pieces += [moving, swap(moving, "fsdp", 1)]
            behind = (ctx - step) % ctx_size
            places += [behind * fsdp_size + fsdp, behind * fsdp_size + (1 - fsdp)]
    else:
        pieces = [lax.all_gather(kv, ("ctx", "fsdp"), axis=0, tiled=True)]
        places = [jnp.int32(0)]
    where = jnp.stack([position] + [place * rows for place in places])
    return attend(where, vertical_blocks, slash_offsets, queries, pieces)


def solution(mesh):
    return jax.shard_map(
        per_device,
        mesh=mesh,
        in_specs=(
            P(("ctx", "fsdp"), "kvh"),
            P("fsdp", "kvh"),
            P(("ctx", "fsdp"), "kvh"),
            P("kvh", None),
            P("kvh", None),
        ),
        out_specs=P(("ctx", "fsdp"), "kvh"),
        check_vma=False,
    )
```

```python
import functools

import jax
import jax.numpy as jnp
from jax import lax
from jax.experimental import pallas as pl
from jax.experimental.pallas import tpu as pltpu
from jax.sharding import PartitionSpec as P


HEAD_DIMENSION = 128
BLOCK_TOKENS = 128
LOG2_E = 1.4426950408889634


ANY = pl.BlockSpec(memory_space=pl.ANY)
VMEM = pl.BlockSpec(memory_space=pltpu.VMEM)
SMEM = pl.BlockSpec(memory_space=pltpu.SMEM)


def swap(value, axis, bit):
    size = lax.axis_size(axis)
    return lax.ppermute(value, axis, [(i, i ^ bit) for i in range(size)])


def rotary_tables(positions):
    half = HEAD_DIMENSION // 2
    frequency = jnp.power(
        500000.0, -(jnp.arange(half, dtype=jnp.float32) * 2.0 / HEAD_DIMENSION)
    )
    angle = positions[:, None] * frequency[None, :]
    cosine = jnp.cos(angle)
    sine = jnp.sin(angle)
    return (
        jnp.concatenate([cosine, cosine], axis=1),
        jnp.concatenate([-sine, sine], axis=1),
    )


def project_kernel(bits, first, last, *refs):
    piece_ref, weight_ref, other_weight_ref = refs[:3]
    rest = refs[3:]
    if not first:
        before_ref, rest = rest[0], rest[1:]
    if last:
        cosine_ref, sine_ref, out_ref, total_ref = rest
    else:
        (total_ref,) = rest
    kvh = lax.axis_index("kvh")
    fsdp = lax.axis_index("fsdp")
    width = piece_ref.shape[1]
    per_half = weight_ref.shape[0] // width
    chunk = kvh ^ jnp.where(fsdp == 0, bits[0], bits[1])
    start = pl.multiple_of((chunk % per_half) * width, width)
    is_own = (chunk // per_half) == fsdp

    def accumulate(weights):
        product = jnp.dot(
            piece_ref[...], weights[pl.ds(start, width), :], preferred_element_type=jnp.float32
        )
        total_ref[...] = product if first else before_ref[...] + product

    @pl.when(is_own)
    def _():
        accumulate(weight_ref)

    @pl.when(jnp.logical_not(is_own))
    def _():
        accumulate(other_weight_ref)

    if not last:
        return
    size = HEAD_DIMENSION
    for head in range(out_ref.shape[1] // (2 * size)):
        at = 2 * head * size
        key = total_ref[:, at : at + size]
        turned = key * cosine_ref[...] + pltpu.roll(key, size // 2, 1) * sine_ref[...]
        out_ref[:, at : at + size] = turned.astype(out_ref.dtype)
        value = total_ref[:, at + size : at + 2 * size]
        out_ref[:, at + size : at + 2 * size] = value.astype(out_ref.dtype)


def project(piece, bits, weights, before=None, tables=None):
    rows = piece.shape[0]
    columns = weights[0].shape[1]
    first = before is None
    last = tables is not None
    operands = [piece, *weights] + ([] if first else [before]) + (list(tables) if last else [])
    part = jax.ShapeDtypeStruct((rows, columns), jnp.float32)
    return pl.pallas_call(
        functools.partial(project_kernel, bits, first, last),
        out_shape=jax.ShapeDtypeStruct((rows, columns), jnp.bfloat16) if last else part,
        in_specs=[VMEM] * len(operands),
        out_specs=VMEM,
        scratch_shapes=[pltpu.VMEM(part.shape, part.dtype)] if last else [],
        compiler_params=pltpu.CompilerParams(vmem_limit_bytes=16 << 20),
        cost_estimate=pl.CostEstimate(
            flops=2 * piece.size * columns,
            bytes_accessed=2 * piece.size + 4 * rows * columns,
            transcendentals=0,
        ),
    )(*operands)


def attend_kernel(
    places, vertical_ref, slash_ref, query_ref, *refs
):
    piece_count = len(places)
    piece_refs = refs[:piece_count]
    out_ref, kv_ref, key_ref, value_ref, sem = refs[piece_count:]
    size = HEAD_DIMENSION
    block = BLOCK_TOKENS
    ctx = lax.axis_index("ctx")
    fsdp = lax.axis_index("fsdp")
    position = ctx * lax.axis_size("fsdp") + fsdp
    local_count = query_ref.shape[0] // block

    def row(place):
        if place is None:
            return 0
        step, flip, local = place
        shard = ((ctx - step) % lax.axis_size("ctx")) * lax.axis_size("fsdp") + (fsdp ^ flip)
        return pl.multiple_of((shard * local_count + local) * block, block)

    copies = [
        pltpu.make_async_copy(
            piece, kv_ref.at[pl.ds(row(place), piece.shape[0])], sem.at[n]
        )
        for n, (piece, place) in enumerate(zip(piece_refs, places))
    ]
    for copy in copies:
        copy.start()
    for copy in copies:
        copy.wait()
    heads = kv_ref.shape[1] // (2 * size)
    group = query_ref.shape[1] // (heads * size)
    vertical_count = vertical_ref.shape[1]
    slash_count = slash_ref.shape[1]
    factor = size ** (-0.5) * LOG2_E
    lower = lax.broadcasted_iota(jnp.int32, (block, block), 1) <= lax.broadcasted_iota(
        jnp.int32, (block, block), 0
    )
    for local in range(local_count):
        mask_block = position * local_count + local
        for head in range(heads):
            offsets = [slash_ref[head, n] for n in range(slash_count)]
            slots = [(mask_block, None)]
            for n in range(vertical_count):
                wanted = vertical_ref[head, n]
                valid = wanted < mask_block
                for offset in offsets:
                    valid = jnp.logical_and(valid, mask_block - wanted != offset)
                slots.append((wanted, valid))
            for offset in offsets:
                valid = offset <= mask_block
                slots.append((jnp.where(valid, mask_block - offset, 0), valid))
            for n, (wanted, _) in enumerate(slots):
                start = pl.multiple_of(wanted * block, block)
                both = kv_ref[pl.ds(start, block), 2 * head * size : 2 * (head + 1) * size]
                key_ref[n * block : (n + 1) * block, :] = both[:, :size]
                value_ref[n * block : (n + 1) * block, :] = both[:, size:]
            bias = [
                None if valid is None else jnp.where(valid, 0.0, -jnp.inf).astype(jnp.float32)
                for _, valid in slots
            ]
            for member in range(group):
                at = (head * group + member) * size
                query = query_ref[local * block : (local + 1) * block, at : at + size]
                scores = lax.dot_general(
                    query, key_ref[...], (((1,), (1,)), ((), ())),
                    preferred_element_type=jnp.float32,
                )
                parts = [
                    jnp.where(lower, scores[:, :block], -jnp.inf)
                    if bias[n] is None
                    else scores[:, n * block : (n + 1) * block] + bias[n]
                    for n in range(len(slots))
                ]
                largest = functools.reduce(jnp.maximum, parts)
                largest = jnp.max(largest, axis=1, keepdims=True) * factor
                expo = [jnp.exp2(part * factor - largest) for part in parts]
                total = jnp.sum(functools.reduce(jnp.add, expo), axis=1, keepdims=True)
                probs = jnp.concatenate([part.astype(jnp.bfloat16) for part in expo], axis=1)
                result = jnp.dot(probs, value_ref[...], preferred_element_type=jnp.float32)
                out_ref[local * block : (local + 1) * block, at : at + size] = (
                    result / total
                ).astype(out_ref.dtype)


def attend(vertical_blocks, slash_offsets, queries, pieces, places):
    rows = queries.shape[0]
    columns = pieces[0].shape[1]
    total_rows = sum(piece.shape[0] for piece in pieces)
    slots = 1 + vertical_blocks.shape[1] + slash_offsets.shape[1]
    keys = slots * BLOCK_TOKENS
    vmem = (16 << 20) + 2 * total_rows * columns
    return pl.pallas_call(
        functools.partial(attend_kernel, places),
        out_shape=jax.ShapeDtypeStruct(queries.shape, jnp.bfloat16),
        in_specs=[SMEM, SMEM, VMEM] + [ANY] * len(pieces),
        out_specs=VMEM,
        scratch_shapes=[
            pltpu.VMEM((total_rows, columns), jnp.bfloat16),
            pltpu.VMEM((keys, HEAD_DIMENSION), jnp.bfloat16),
            pltpu.VMEM((keys, HEAD_DIMENSION), jnp.bfloat16),
            pltpu.SemaphoreType.DMA((len(pieces),)),
        ],
        compiler_params=pltpu.CompilerParams(vmem_limit_bytes=vmem),
        cost_estimate=pl.CostEstimate(
            flops=4 * rows * queries.shape[1] * keys,
            bytes_accessed=2 * total_rows * columns + 4 * queries.size,
            transcendentals=rows * keys * queries.shape[1] // HEAD_DIMENSION,
        ),
    )(vertical_blocks, slash_offsets, queries, *pieces)


def phase_kernel(
    count, places, first, last, vertical_ref, slash_ref, query_ref, *refs
):
    pieces, refs = refs[:count], refs[count:]
    if first:
        total_ref, largest_ref, mass_ref = refs
    elif last:
        before_total, before_largest, before_mass, out_ref = refs
    else:
        before_total, before_largest, before_mass, total_ref, largest_ref, mass_ref = refs
    size = HEAD_DIMENSION
    block = BLOCK_TOKENS
    ctx = lax.axis_index("ctx")
    fsdp = lax.axis_index("fsdp")
    fsdp_size = lax.axis_size("fsdp")
    local_count = query_ref.shape[0] // block
    heads = pieces[0].shape[1] // (2 * size)
    group = query_ref.shape[1] // (heads * size)
    wide = group * block
    factor = size ** (-0.5) * LOG2_E
    lower = lax.broadcasted_iota(jnp.int32, (block, wide), 0) <= (
        lax.broadcasted_iota(jnp.int32, (block, wide), 1) % block
    )
    position = ctx * fsdp_size + fsdp
    places = [(step, flip, local) for step, flip in places for local in range(local_count)]
    pieces = [
        piece.at[local * block : (local + 1) * block] for piece in pieces for local in range(local_count)
    ]
    for head in range(heads):
        at_key = 2 * head * size
        vertical = [vertical_ref[head, n] for n in range(vertical_ref.shape[1])]
        offsets = [slash_ref[head, n] for n in range(slash_ref.shape[1])]
        wanted = {}
        for step, flip, local in places:
            shard = (ctx ^ step) * fsdp_size + (fsdp ^ flip)
            key_block = shard * local_count + local
            hit = functools.reduce(jnp.logical_or, [key_block == v for v in vertical])
            wanted[step, flip, local] = (key_block, hit)
        for here in range(local_count):
            mask_block = position * local_count + here
            at = head * group * size
            rows = slice(here * block, (here + 1) * block)
            query = jnp.concatenate(
                [query_ref[rows, at + g * size : at + (g + 1) * size] for g in range(group)], axis=0
            )
            scores, biases, values = [], [], []
            for piece, place in zip(pieces, places):
                step, flip, local = place
                own = step == 0 and flip == 0
                if own and local > here:
                    continue
                score = lax.dot_general(
                    piece[:, at_key : at_key + size], query, (((1,), (1,)), ((), ())),
                    preferred_element_type=jnp.float32,
                )
                values.append(piece[:, at_key + size : at_key + 2 * size])
                if own and local == here:
                    scores.append(jnp.where(lower, score, -jnp.inf))
                    biases.append(None)
                    continue
                key_block, hit = wanted[place]
                slash = functools.reduce(
                    jnp.logical_or, [mask_block - key_block == offset for offset in offsets]
                )
                valid = jnp.logical_and(key_block < mask_block, jnp.logical_or(hit, slash))
                scores.append(score)
                biases.append(jnp.where(valid, 0.0, -jnp.inf).astype(jnp.float32))
            combo = head * local_count + here
            tops = []
            for score, bias in zip(scores, biases):
                top = jnp.max(score.reshape(block // 8, 8, wide), axis=0)
                tops.append(top if bias is None else top + bias)
            largest = jnp.max(functools.reduce(jnp.maximum, tops), axis=0, keepdims=True) * factor
            if not first:
                before = before_largest[combo]
                largest = jnp.maximum(largest, before)
                shrink = jnp.exp2(before - largest)
            expo = [
                jnp.exp2(score * factor - (largest if bias is None else largest - bias))
                for score, bias in zip(scores, biases)
            ]
            mass = functools.reduce(
                jnp.add, [part.reshape(block // 8, 8, wide).sum(axis=0) for part in expo]
            ).sum(axis=0, keepdims=True)
            probs = jnp.concatenate([part.astype(jnp.bfloat16) for part in expo], axis=0)
            total = lax.dot_general(
                jnp.concatenate(values, axis=0), probs, (((0,), (0,)), ((), ())),
                preferred_element_type=jnp.float32,
            )
            if not first:
                mass = mass + before_mass[combo] * shrink
                total = total + before_total[combo] * shrink
            if not last:
                total_ref[combo] = total
                largest_ref[combo] = largest
                mass_ref[combo] = mass
                continue
            result = (total / mass).T
            for g in range(group):
                out_ref[rows, at + g * size : at + (g + 1) * size] = result[
                    g * block : (g + 1) * block
                ].astype(out_ref.dtype)


def attend_phase(vertical_blocks, slash_offsets, queries, pieces, places, before, last):
    rows = queries.shape[0]
    heads = vertical_blocks.shape[0]
    size = HEAD_DIMENSION
    group = queries.shape[1] // (heads * size)
    combos = heads * rows // BLOCK_TOKENS
    wide = group * BLOCK_TOKENS
    state = (
        jax.ShapeDtypeStruct((combos, size, wide), jnp.float32),
        jax.ShapeDtypeStruct((combos, 1, wide), jnp.float32),
        jax.ShapeDtypeStruct((combos, 1, wide), jnp.float32),
    )
    keys = len(pieces) * rows
    return pl.pallas_call(
        functools.partial(phase_kernel, len(pieces), places, before is None, last),
        out_shape=jax.ShapeDtypeStruct(queries.shape, jnp.bfloat16) if last else state,
        in_specs=[SMEM, SMEM] + [VMEM] * (1 + len(pieces) + (0 if before is None else 3)),
        out_specs=VMEM if last else (VMEM,) * 3,
        compiler_params=pltpu.CompilerParams(vmem_limit_bytes=24 << 20),
        cost_estimate=pl.CostEstimate(
            flops=4 * rows * queries.shape[1] * keys,
            bytes_accessed=4 * queries.size,
            transcendentals=rows * keys * queries.shape[1] // size,
        ),
    )(vertical_blocks, slash_offsets, queries, *pieces, *(before or ()))


def per_device(hidden, key_value_matrix, queries, vertical_blocks, slash_offsets):
    rows = hidden.shape[0]
    kvh_size = lax.axis_size("kvh")
    position = lax.axis_index(("ctx", "fsdp"))

    def hop(value, bits):
        pairs = [
            (core * kvh_size + k, core * kvh_size + (k ^ bits[core]))
            for core in range(lax.axis_size("fsdp"))
            for k in range(kvh_size)
        ]
        return lax.ppermute(value, ("fsdp", "kvh"), pairs)

    other_weight = swap(key_value_matrix, "fsdp", 1)
    one = hop(hidden, (1, 2))
    two = hop(hidden, (2, 1))
    three = hop(one, (2, 1))

    positions = (position * rows + jnp.arange(rows, dtype=jnp.int32)).astype(jnp.float32)
    tables = rotary_tables(positions)
    weights = (key_value_matrix, other_weight)
    total = project(hidden, (0, 0), weights)
    total = project(one, (1, 2), weights, total)
    total = project(two, (2, 1), weights, total)
    own = project(three, (3, 3), weights, total, tables)
    if lax.axis_size("ctx") != 4:
        pieces = [lax.all_gather(own, ("ctx", "fsdp"), axis=0, tiled=True)]
        return attend(vertical_blocks, slash_offsets, queries, pieces, [None])

    def both(moved):
        return [moved, swap(moved, "fsdp", 1)]

    def places(*steps):
        return [(step, flip) for step in steps for flip in (0, 1)]

    far = swap(own, "ctx", 2)
    near = swap(own, "ctx", 1)
    late = swap(own, "ctx", 3)
    masks = (vertical_blocks, slash_offsets, queries)
    state = attend_phase(*masks, both(own), places(0), None, False)
    state = attend_phase(*masks, both(near) + both(far), places(1, 2), state, False)
    return attend_phase(*masks, both(late), places(3), state, True)


def solution(mesh):
    return jax.shard_map(
        per_device,
        mesh=mesh,
        in_specs=(
            P(("ctx", "fsdp"), "kvh"),
            P("fsdp", "kvh"),
            P(("ctx", "fsdp"), "kvh"),
            P("kvh", None),
            P("kvh", None),
        ),
        out_specs=P(("ctx", "fsdp"), "kvh"),
        check_vma=False,
    )
```

```python
import functools

import jax
import jax.numpy as jnp
from jax import lax
from jax.experimental import pallas as pl
from jax.experimental.pallas import tpu as pltpu
from jax.sharding import PartitionSpec as P


HEAD_DIMENSION = 128
BLOCK_TOKENS = 128
LOG2_E = 1.4426950408889634


ANY = pl.BlockSpec(memory_space=pl.ANY)
VMEM = pl.BlockSpec(memory_space=pltpu.VMEM)
SMEM = pl.BlockSpec(memory_space=pltpu.SMEM)


def swap(value, axis, bit):
    size = lax.axis_size(axis)
    return lax.ppermute(value, axis, [(i, i ^ bit) for i in range(size)])


def rotary_tables(positions):
    half = HEAD_DIMENSION // 2
    frequency = jnp.power(
        500000.0, -(jnp.arange(half, dtype=jnp.float32) * 2.0 / HEAD_DIMENSION)
    )
    angle = positions[:, None] * frequency[None, :]
    cosine = jnp.cos(angle)
    sine = jnp.sin(angle)
    return (
        jnp.concatenate([cosine, cosine], axis=1),
        jnp.concatenate([-sine, sine], axis=1),
    )


def project_kernel(bits, first, last, *refs):
    piece_ref, weight_ref, other_weight_ref = refs[:3]
    rest = refs[3:]
    if not first:
        before_ref, rest = rest[0], rest[1:]
    if last:
        cosine_ref, sine_ref, out_ref, total_ref = rest
    else:
        (total_ref,) = rest
    kvh = lax.axis_index("kvh")
    fsdp = lax.axis_index("fsdp")
    width = piece_ref.shape[1]
    per_half = weight_ref.shape[0] // width
    chunk = kvh ^ jnp.where(fsdp == 0, bits[0], bits[1])
    start = pl.multiple_of((chunk % per_half) * width, width)
    is_own = (chunk // per_half) == fsdp

    def accumulate(weights):
        product = jnp.dot(
            piece_ref[...], weights[pl.ds(start, width), :], preferred_element_type=jnp.float32
        )
        total_ref[...] = product if first else before_ref[...] + product

    @pl.when(is_own)
    def _():
        accumulate(weight_ref)

    @pl.when(jnp.logical_not(is_own))
    def _():
        accumulate(other_weight_ref)

    if not last:
        return
    size = HEAD_DIMENSION
    for head in range(out_ref.shape[1] // (2 * size)):
        at = 2 * head * size
        key = total_ref[:, at : at + size]
        turned = key * cosine_ref[...] + pltpu.roll(key, size // 2, 1) * sine_ref[...]
        out_ref[:, at : at + size] = turned.astype(out_ref.dtype)
        value = total_ref[:, at + size : at + 2 * size]
        out_ref[:, at + size : at + 2 * size] = value.astype(out_ref.dtype)


def project(piece, bits, weights, before=None, tables=None):
    rows = piece.shape[0]
    columns = weights[0].shape[1]
    first = before is None
    last = tables is not None
    operands = [piece, *weights] + ([] if first else [before]) + (list(tables) if last else [])
    part = jax.ShapeDtypeStruct((rows, columns), jnp.float32)
    return pl.pallas_call(
        functools.partial(project_kernel, bits, first, last),
        out_shape=jax.ShapeDtypeStruct((rows, columns), jnp.bfloat16) if last else part,
        in_specs=[VMEM] * len(operands),
        out_specs=VMEM,
        scratch_shapes=[pltpu.VMEM(part.shape, part.dtype)] if last else [],
        compiler_params=pltpu.CompilerParams(vmem_limit_bytes=16 << 20),
        cost_estimate=pl.CostEstimate(
            flops=2 * piece.size * columns,
            bytes_accessed=2 * piece.size + 4 * rows * columns,
            transcendentals=0,
        ),
    )(*operands)


def attend_kernel(
    places, vertical_ref, slash_ref, query_ref, *refs
):
    piece_count = len(places)
    piece_refs = refs[:piece_count]
    out_ref, kv_ref, key_ref, value_ref, sem = refs[piece_count:]
    size = HEAD_DIMENSION
    block = BLOCK_TOKENS
    ctx = lax.axis_index("ctx")
    fsdp = lax.axis_index("fsdp")
    position = ctx * lax.axis_size("fsdp") + fsdp
    local_count = query_ref.shape[0] // block

    def row(place):
        if place is None:
            return 0
        step, flip, local = place
        shard = ((ctx - step) % lax.axis_size("ctx")) * lax.axis_size("fsdp") + (fsdp ^ flip)
        return pl.multiple_of((shard * local_count + local) * block, block)

    copies = [
        pltpu.make_async_copy(
            piece, kv_ref.at[pl.ds(row(place), piece.shape[0])], sem.at[n]
        )
        for n, (piece, place) in enumerate(zip(piece_refs, places))
    ]
    for copy in copies:
        copy.start()
    for copy in copies:
        copy.wait()
    heads = kv_ref.shape[1] // (2 * size)
    group = query_ref.shape[1] // (heads * size)
    vertical_count = vertical_ref.shape[1]
    slash_count = slash_ref.shape[1]
    factor = size ** (-0.5) * LOG2_E
    lower = lax.broadcasted_iota(jnp.int32, (block, block), 1) <= lax.broadcasted_iota(
        jnp.int32, (block, block), 0
    )
    for local in range(local_count):
        mask_block = position * local_count + local
        for head in range(heads):
            offsets = [slash_ref[head, n] for n in range(slash_count)]
            slots = [(mask_block, None)]
            for n in range(vertical_count):
                wanted = vertical_ref[head, n]
                valid = wanted < mask_block
                for offset in offsets:
                    valid = jnp.logical_and(valid, mask_block - wanted != offset)
                slots.append((wanted, valid))
            for offset in offsets:
                valid = offset <= mask_block
                slots.append((jnp.where(valid, mask_block - offset, 0), valid))
            for n, (wanted, _) in enumerate(slots):
                start = pl.multiple_of(wanted * block, block)
                both = kv_ref[pl.ds(start, block), 2 * head * size : 2 * (head + 1) * size]
                key_ref[n * block : (n + 1) * block, :] = both[:, :size]
                value_ref[n * block : (n + 1) * block, :] = both[:, size:]
            bias = [
                None if valid is None else jnp.where(valid, 0.0, -jnp.inf).astype(jnp.float32)
                for _, valid in slots
            ]
            for member in range(group):
                at = (head * group + member) * size
                query = query_ref[local * block : (local + 1) * block, at : at + size]
                scores = lax.dot_general(
                    query, key_ref[...], (((1,), (1,)), ((), ())),
                    preferred_element_type=jnp.float32,
                )
                parts = [
                    jnp.where(lower, scores[:, :block], -jnp.inf)
                    if bias[n] is None
                    else scores[:, n * block : (n + 1) * block] + bias[n]
                    for n in range(len(slots))
                ]
                largest = functools.reduce(jnp.maximum, parts)
                largest = jnp.max(largest, axis=1, keepdims=True) * factor
                expo = [jnp.exp2(part * factor - largest) for part in parts]
                total = jnp.sum(functools.reduce(jnp.add, expo), axis=1, keepdims=True)
                probs = jnp.concatenate([part.astype(jnp.bfloat16) for part in expo], axis=1)
                result = jnp.dot(probs, value_ref[...], preferred_element_type=jnp.float32)
                out_ref[local * block : (local + 1) * block, at : at + size] = (
                    result / total
                ).astype(out_ref.dtype)


def attend(vertical_blocks, slash_offsets, queries, pieces, places):
    rows = queries.shape[0]
    columns = pieces[0].shape[1]
    total_rows = sum(piece.shape[0] for piece in pieces)
    slots = 1 + vertical_blocks.shape[1] + slash_offsets.shape[1]
    keys = slots * BLOCK_TOKENS
    vmem = (16 << 20) + 2 * total_rows * columns
    return pl.pallas_call(
        functools.partial(attend_kernel, places),
        out_shape=jax.ShapeDtypeStruct(queries.shape, jnp.bfloat16),
        in_specs=[SMEM, SMEM, VMEM] + [ANY] * len(pieces),
        out_specs=VMEM,
        scratch_shapes=[
            pltpu.VMEM((total_rows, columns), jnp.bfloat16),
            pltpu.VMEM((keys, HEAD_DIMENSION), jnp.bfloat16),
            pltpu.VMEM((keys, HEAD_DIMENSION), jnp.bfloat16),
            pltpu.SemaphoreType.DMA((len(pieces),)),
        ],
        compiler_params=pltpu.CompilerParams(vmem_limit_bytes=vmem),
        cost_estimate=pl.CostEstimate(
            flops=4 * rows * queries.shape[1] * keys,
            bytes_accessed=2 * total_rows * columns + 4 * queries.size,
            transcendentals=rows * keys * queries.shape[1] // HEAD_DIMENSION,
        ),
    )(vertical_blocks, slash_offsets, queries, *pieces)


def phase_kernel(
    count, places, first, last, vertical_ref, slash_ref, query_ref, *refs
):
    pieces, refs = refs[:count], refs[count:]
    if first:
        total_ref, largest_ref, mass_ref = refs
    elif last:
        before_total, before_largest, before_mass, out_ref = refs
    else:
        before_total, before_largest, before_mass, total_ref, largest_ref, mass_ref = refs
    size = HEAD_DIMENSION
    block = BLOCK_TOKENS
    ctx = lax.axis_index("ctx")
    fsdp = lax.axis_index("fsdp")
    fsdp_size = lax.axis_size("fsdp")
    local_count = query_ref.shape[0] // block
    heads = pieces[0].shape[1] // (2 * size)
    group = query_ref.shape[1] // (heads * size)
    wide = group * block
    factor = size ** (-0.5) * LOG2_E
    lower = lax.broadcasted_iota(jnp.int32, (block, wide), 0) <= (
        lax.broadcasted_iota(jnp.int32, (block, wide), 1) % block
    )
    position = ctx * fsdp_size + fsdp

    def finish(combo, total, mass):
        head, here = combo // local_count, combo % local_count
        at = head * group * size
        result = (total / mass).astype(out_ref.dtype).T
        for g in range(group):
            out_ref[here * block : (here + 1) * block, at + g * size : at + (g + 1) * size] = (
                result[g * block : (g + 1) * block]
            )

    def attend_all(places, pieces):
        places = [(step, flip, local) for step, flip in places for local in range(local_count)]
        pieces = [
            piece.at[local * block : (local + 1) * block] for piece in pieces for local in range(local_count)
        ]
        for head in range(heads):
            at_key = 2 * head * size
            vertical = [vertical_ref[head, n] for n in range(vertical_ref.shape[1])]
            offsets = [slash_ref[head, n] for n in range(slash_ref.shape[1])]
            wanted = {}
            for step, flip, local in places:
                shard = (ctx - step) * fsdp_size + (fsdp ^ flip)
                key_block = shard * local_count + local
                hit = functools.reduce(jnp.logical_or, [key_block == v for v in vertical])
                near = key_block >= 0
                wanted[step, flip, local] = (key_block, hit, near)
            for here in range(local_count):
                mask_block = position * local_count + here
                at = head * group * size
                rows = slice(here * block, (here + 1) * block)
                query = jnp.concatenate(
                    [query_ref[rows, at + g * size : at + (g + 1) * size] for g in range(group)], axis=0
                )
                scores, biases, values = [], [], []
                for piece, place in zip(pieces, places):
                    step, flip, local = place
                    own = step == 0 and flip == 0
                    if own and local > here:
                        continue
                    score = lax.dot_general(
                        piece[:, at_key : at_key + size], query, (((1,), (1,)), ((), ())),
                        preferred_element_type=jnp.float32,
                    )
                    values.append(piece[:, at_key + size : at_key + 2 * size])
                    if own and local == here:
                        scores.append(jnp.where(lower, score, -jnp.inf))
                        biases.append(None)
                        continue
                    key_block, hit, near = wanted[place]
                    slash = functools.reduce(
                        jnp.logical_or, [mask_block - key_block == offset for offset in offsets]
                    )
                    valid = jnp.logical_and(
                        jnp.logical_and(near, key_block < mask_block), jnp.logical_or(hit, slash)
                    )
                    scores.append(score)
                    biases.append(jnp.where(valid, 0.0, -jnp.inf).astype(jnp.float32))
                combo = head * local_count + here
                tops = []
                for score, bias in zip(scores, biases):
                    top = jnp.max(score.reshape(block // 8, 8, wide), axis=0)
                    tops.append(top if bias is None else top + bias)
                largest = jnp.max(functools.reduce(jnp.maximum, tops), axis=0, keepdims=True) * factor
                if not first:
                    before = before_largest[combo]
                    largest = jnp.maximum(largest, before)
                    shrink = jnp.exp2(before - largest)
                expo = [
                    jnp.exp2(score * factor - (largest if bias is None else largest - bias))
                    for score, bias in zip(scores, biases)
                ]
                mass = functools.reduce(
                    jnp.add, [part.reshape(block // 8, 8, wide).sum(axis=0) for part in expo]
                ).sum(axis=0, keepdims=True)
                probs = jnp.concatenate([part.astype(jnp.bfloat16) for part in expo], axis=0)
                total = lax.dot_general(
                    jnp.concatenate(values, axis=0), probs, (((0,), (0,)), ((), ())),
                    preferred_element_type=jnp.float32,
                )
                if not first:
                    mass = mass + before_mass[combo] * shrink
                    total = total + before_total[combo] * shrink
                if not last:
                    total_ref[combo] = total
                    largest_ref[combo] = largest
                    mass_ref[combo] = mass
                    continue
                finish(combo, total, mass)

    if first:
        attend_all(places, pieces)
        return
    active = functools.reduce(jnp.logical_or, [ctx >= step for step, _ in places])

    @pl.when(active)
    def _():
        attend_all(places, pieces)

    @pl.when(jnp.logical_not(active))
    def _():
        for combo in range(before_mass.shape[0]):
            if last:
                finish(combo, before_total[combo], before_mass[combo])
            else:
                total_ref[combo] = before_total[combo]
                largest_ref[combo] = before_largest[combo]
                mass_ref[combo] = before_mass[combo]


def attend_phase(vertical_blocks, slash_offsets, queries, pieces, places, before, last):
    rows = queries.shape[0]
    heads = vertical_blocks.shape[0]
    size = HEAD_DIMENSION
    group = queries.shape[1] // (heads * size)
    combos = heads * rows // BLOCK_TOKENS
    wide = group * BLOCK_TOKENS
    state = (
        jax.ShapeDtypeStruct((combos, size, wide), jnp.float32),
        jax.ShapeDtypeStruct((combos, 1, wide), jnp.float32),
        jax.ShapeDtypeStruct((combos, 1, wide), jnp.float32),
    )
    keys = len(pieces) * rows
    return pl.pallas_call(
        functools.partial(phase_kernel, len(pieces), places, before is None, last),
        out_shape=jax.ShapeDtypeStruct(queries.shape, jnp.bfloat16) if last else state,
        in_specs=[SMEM, SMEM] + [VMEM] * (1 + len(pieces) + (0 if before is None else 3)),
        out_specs=VMEM if last else (VMEM,) * 3,
        compiler_params=pltpu.CompilerParams(vmem_limit_bytes=24 << 20),
        cost_estimate=pl.CostEstimate(
            flops=4 * rows * queries.shape[1] * keys,
            bytes_accessed=4 * queries.size,
            transcendentals=rows * keys * queries.shape[1] // size,
        ),
    )(vertical_blocks, slash_offsets, queries, *pieces, *(before or ()))


def per_device(hidden, key_value_matrix, queries, vertical_blocks, slash_offsets):
    rows = hidden.shape[0]
    kvh_size = lax.axis_size("kvh")
    position = lax.axis_index(("ctx", "fsdp"))

    def hop(value, bits):
        pairs = [
            (core * kvh_size + k, core * kvh_size + (k ^ bits[core]))
            for core in range(lax.axis_size("fsdp"))
            for k in range(kvh_size)
        ]
        return lax.ppermute(value, ("fsdp", "kvh"), pairs)

    other_weight = swap(key_value_matrix, "fsdp", 1)
    one = hop(hidden, (1, 2))
    two = hop(hidden, (2, 1))
    three = hop(one, (2, 1))

    positions = (position * rows + jnp.arange(rows, dtype=jnp.int32)).astype(jnp.float32)
    tables = rotary_tables(positions)
    weights = (key_value_matrix, other_weight)
    total = project(hidden, (0, 0), weights)
    total = project(one, (1, 2), weights, total)
    total = project(two, (2, 1), weights, total)
    own = project(three, (3, 3), weights, total, tables)
    if lax.axis_size("ctx") != 4:
        pieces = [lax.all_gather(own, ("ctx", "fsdp"), axis=0, tiled=True)]
        return attend(vertical_blocks, slash_offsets, queries, pieces, [None])

    def both(moved):
        return [moved, swap(moved, "fsdp", 1)]

    def places(*steps):
        return [(step, flip) for step in steps for flip in (0, 1)]

    behind = lax.ppermute(own, "ctx", [(i, (i + 1) % 4) for i in range(4)])
    last = lax.ppermute(own, "ctx", [(0, 3)])
    behind_two = lax.ppermute(behind, "ctx", [(i, (i + 1) % 4) for i in range(4)])
    last_pair = both(last)
    behind_pair = both(behind)
    masks = (vertical_blocks, slash_offsets, queries)
    state = attend_phase(*masks, both(own), places(0), None, False)
    state = attend_phase(*masks, behind_pair, places(1), state, False)
    state = attend_phase(*masks, last_pair, places(3), state, False)
    return attend_phase(*masks, both(behind_two), places(2), state, True)


def solution(mesh):
    return jax.shard_map(
        per_device,
        mesh=mesh,
        in_specs=(
            P(("ctx", "fsdp"), "kvh"),
            P("fsdp", "kvh"),
            P(("ctx", "fsdp"), "kvh"),
            P("kvh", None),
            P("kvh", None),
        ),
        out_specs=P(("ctx", "fsdp"), "kvh"),
        check_vma=False,
    )
```
